32 devices in a mesh: dp: 8 (over z, y), tensor: 4 (over x, core).
Axes of the slice: x: 2, y: 2, z: 4, core: 2. Of those that a mesh axis runs over, the one named last changes fastest.
Arguments:
- states: bfloat16 [8192, 1536], P(('dp', 'tensor')), may hold values from -6 to 6
- cotangent: bfloat16 [8192, 1536], P(('dp', 'tensor')), may hold values from -6 to 6
- teacher: bfloat16 [8192, 1536], P(('dp', 'tensor')), may hold values from -9 to 9
- prefix_len: int32 [8], P('dp'), may hold values from 102 to 512
- validity: int32 [8, 1024], P('dp'), may hold values from 0 to 1, as said below
- w_query: bfloat16 [1536, 1536], P('dp', 'tensor'), may hold values from -0.15625 to 0.15625
- key_projection_weight: bfloat16 [1536, 256], P(('dp', 'tensor')), may hold values from -0.15625 to 0.15625
- value_projection_weight: bfloat16 [1536, 256], P(('dp', 'tensor')), may hold values from -0.15625 to 0.15625
- w_output: bfloat16 [1536, 1536], P('tensor', 'dp'), may hold values from -2.5 to 2.5
- w_gate: bfloat16 [1536, 8960], P('dp', 'tensor'), may hold values from -0.15625 to 0.15625
- w_up: bfloat16 [1536, 8960], P('dp', 'tensor'), may hold values from -0.15625 to 0.15625
- w_down: bfloat16 [8960, 1536], P('tensor', 'dp'), may hold values from -0.0625 to 0.0625
- b_query: bfloat16 [1536], P(('dp', 'tensor')), may hold values from -3 to 3
- key_offset_bias: bfloat16 [256], P(('dp', 'tensor')), may hold values from -3 to 3
- value_offset_bias: bfloat16 [256], P(('dp', 'tensor')), may hold values from -0.059814453 to 0.059814453
- gain_attn: bfloat16 [1536], P(('dp', 'tensor')), may hold values from 0.5 to 1.5
- gain_ffn: bfloat16 [1536], P(('dp', 'tensor')), may hold values from 0.5 to 1.5
Outputs:
- layer_out: bfloat16 [8192, 1536], P(('dp', 'tensor'))
- distill_loss: float32 [], replicated
- grad_states: float32 [8192, 1536], P(('dp', 'tensor'))
- grad_w_query: float32 [1536, 1536], P('dp', 'tensor')
- grad_w_key: float32 [1536, 256], P(('dp', 'tensor'))
- grad_w_value: float32 [1536, 256], P(('dp', 'tensor'))
- grad_w_output: float32 [1536, 1536], P('tensor', 'dp')
- grad_w_gate: float32 [1536, 8960], P('dp', 'tensor')
- grad_w_up: float32 [1536, 8960], P('dp', 'tensor')
- grad_w_down: float32 [8960, 1536], P('tensor', 'dp')
- grad_b_query: float32 [1536], P(('dp', 'tensor'))
- grad_b_key: float32 [256], P(('dp', 'tensor'))
- grad_b_value: float32 [256], P(('dp', 'tensor'))
- grad_gain_attn: float32 [1536], P(('dp', 'tensor'))
- grad_gain_ffn: float32 [1536], P(('dp', 'tensor'))
The draws below stay inside these ranges and needn't reach their ends.
Inputs may be any that keep to these rules, and one draw needn't show every extreme that they name: `validity`: the first token of every sequence is real.
All inputs are finite; a program needn't handle non-finite values.
Results may differ from the reference program's by a relative error of at most 0.017.
Values may be sent and summed in bfloat16 or wider, within the bound.
No kernel may reach another device: no remote copies, remote signals or barrier semaphores. Data moves between devices by JAX's collectives and lax.ppermute only.
A program may use at most 192 MiB of HBM per device.

```python
import jax
import jax.numpy as jnp
import numpy as np
from jax import lax

MODEL_WIDTH = 1536
QUERY_HEADS = 12
KEY_VALUE_HEADS = 2
HEAD_SIZE = 128
FF = 8960
LEN = 1024
SEQS = 8
TOKENS = 8192
QUERY_PER_SHARD = 3
N_TENSOR = 4


def draw_validity(key, part):
    seq_ids = jnp.arange(SEQS, dtype=jnp.int32)[:, None]
    rolled = jax.random.randint(key, (SEQS, LEN), 0, 3 * SEQS, dtype=jnp.int32)
    kept = (rolled < SEQS + 2 * seq_ids).astype(jnp.int32)
    leading = (jnp.arange(LEN, dtype=jnp.int32) == 0).astype(jnp.int32)[None, :]
    return jnp.maximum(kept, leading)


def place_ends(entries, rng, low, top_value):
    place = [jax.random.randint(jax.random.fold_in(rng, axis), (), 0, length) for axis, length in enumerate(entries.shape)]
    main_axis = entries.shape.index(max(entries.shape))
    neighbour = place[:main_axis] + [(place[main_axis] + 1) % entries.shape[main_axis]] + place[main_axis + 1:]
    return entries.at[tuple(place)].set(low).at[tuple(neighbour)].set(top_value)


def levels(stream_key, extent, cuts, low, largest):
    def one(position, blocks):
        steps = jax.random.uniform(jax.random.fold_in(jax.random.fold_in(stream_key, 6), position), (blocks,), jnp.float32, low / len(cuts), largest / len(cuts))
        return jnp.repeat(jnp.exp(steps), extent[position] // blocks).reshape((-1,) + (1,) * (len(extent) - position - 1))

    level = one(*cuts[0])
    for cut in cuts[1:]:
        level = level * one(*cut)
    return level


def scatter_about(own_key, dims, spread, bound, cuts=(), kind=jnp.bfloat16):
    array = jax.random.normal(own_key, dims, jnp.float32) * spread
    if len(cuts) > 0:
        array = levels(own_key, dims, cuts, -0.22, 0.18) * array
    return jnp.clip(array, min=-bound, max=bound).astype(kind)


def setup_inputs(seed: int = 0) -> dict:
    seeds = jax.random.split(jax.random.key(seed), 18)
    return {
        "states": scatter_about(seeds[0], (TOKENS, MODEL_WIDTH), 1.0, 6.0, ((0, 32),)),
        "cotangent": scatter_about(seeds[1], (TOKENS, MODEL_WIDTH), 1.0, 6.0, ((0, 32),)),
        "teacher": scatter_about(seeds[2], (TOKENS, MODEL_WIDTH), 1.5, 9.0, ((0, 32),)),
        "prefix_len": place_ends(jax.random.randint(seeds[3], (SEQS,), LEN // 10, LEN // 2 + 1), jax.random.fold_in(seeds[3], 1), LEN // 10, (LEN // 2 + 1) - 1).astype(jnp.int32),
        "validity": draw_validity(jax.random.fold_in(seeds[17], 71), 0),
        "w_query": scatter_about(seeds[5], (MODEL_WIDTH, QUERY_HEADS * HEAD_SIZE), MODEL_WIDTH ** -0.5, 0.15625, ((0, 8), (1, 4))),
        "key_projection_weight": scatter_about(seeds[6], (MODEL_WIDTH, KEY_VALUE_HEADS * HEAD_SIZE), MODEL_WIDTH ** -0.5, 0.15625, ((0, 32),)),
        "value_projection_weight": scatter_about(seeds[7], (MODEL_WIDTH, KEY_VALUE_HEADS * HEAD_SIZE), MODEL_WIDTH ** -0.5, 0.15625, ((0, 32),)),
        "w_output": scatter_about(seeds[8], (QUERY_HEADS * HEAD_SIZE, MODEL_WIDTH), (QUERY_HEADS * HEAD_SIZE // 256) ** -0.5, 2.5, ((0, 4), (1, 8))),
        "w_gate": scatter_about(seeds[9], (MODEL_WIDTH, FF), MODEL_WIDTH ** -0.5, 0.15625, ((0, 8), (1, 4))),
        "w_up": scatter_about(seeds[10], (MODEL_WIDTH, FF), MODEL_WIDTH ** -0.5, 0.15625, ((0, 8), (1, 4))),
        "w_down": scatter_about(seeds[11], (FF, MODEL_WIDTH), FF ** -0.5, 0.0625, ((0, 4), (1, 8))),
        "b_query": scatter_about(seeds[12], (QUERY_HEADS * HEAD_SIZE,), 0.5, 3.0, ((0, 32),)),
        "key_offset_bias": scatter_about(seeds[13], (KEY_VALUE_HEADS * HEAD_SIZE,), 0.5, 3.0, ((0, 32),)),
        "value_offset_bias": scatter_about(seeds[14], (KEY_VALUE_HEADS * HEAD_SIZE,), 0.02, 0.059814453, ((0, 32),)),
        "gain_attn": jnp.clip(1.0 + 0.1 * jax.random.normal(seeds[15], (MODEL_WIDTH,), jnp.float32), 0.5, 1.5).astype(jnp.bfloat16),
        "gain_ffn": jnp.clip(1.0 + 0.1 * jax.random.normal(seeds[16], (MODEL_WIDTH,), jnp.float32), 0.5, 1.5).astype(jnp.bfloat16),
    }


NORM_EPS = 1e-06
ROPE_BASE = 10000.0
NEG_FILL = -1e+30
HIGHEST = lax.Precision.HIGHEST

@jax.custom_vjp
def low(v):
    return lax.optimization_barrier(v.astype(jnp.bfloat16)).astype(jnp.float32)

@jax.custom_vjp
def low_back(v):
    return v

def low_keep(v):
    return (low(v), None)

def low_pass(kept, grad):
    return (grad,)

def back_keep(v):
    return (v, None)

def back_low(kept, grad):
    return (low(grad),)
low.defvjp(low_keep, low_pass)
low_back.defvjp(back_keep, back_low)

def tables(sequence_length, head_width):
    half_width = head_width // 2
    inverse = ROPE_BASE ** (-(jnp.arange(half_width, dtype=jnp.float32) * 2.0 / head_width))
    angles = jnp.arange(sequence_length, dtype=jnp.float32)[:, None] * inverse[None, :]
    return (jnp.cos(angles), jnp.sin(angles))

def rotate(values, cosine, sine):
    half_width = values.shape[-1] // 2
    first = values[..., :half_width]
    second = values[..., half_width:]
    return jnp.concatenate([first * cosine - second * sine, second * cosine + first * sine], axis=-1)

def norm_rows(values, gain):
    return values * lax.rsqrt(lax.optimization_barrier(jnp.mean(values * values, -1, keepdims=True)) + NORM_EPS) * gain

def allowed_keys(query_pos, sequence_length, prefix, valid):
    key_pos = jnp.arange(sequence_length, dtype=jnp.int32)
    causal = key_pos[None, :] <= query_pos[:, None]
    return (causal | (key_pos[None, :] < prefix)) & (valid[None, :] > 0)

def matrix_product(left, right):
    return jnp.dot(left, right, precision=HIGHEST, preferred_element_type=jnp.float32)

def sequence_layer(params, states, valid, prefix, cosine, sine):
    w_query, key_projection_weight, value_projection_weight, w_output, w_gate, w_up, w_down, b_query, key_offset_bias, value_offset_bias, gain_attn, gain_ffn = params
    sequence_length = states.shape[0]
    replica_count = np.arange(N_TENSOR) * QUERY_PER_SHARD // (QUERY_HEADS // KEY_VALUE_HEADS)
    normalized_rows = low(norm_rows(states, gain_attn))
    query_raw = low_back((matrix_product(normalized_rows, w_query) + b_query).reshape(sequence_length, QUERY_HEADS, HEAD_SIZE))
    key_everything = (matrix_product(normalized_rows, key_projection_weight) + key_offset_bias).reshape(sequence_length, KEY_VALUE_HEADS, HEAD_SIZE)
    value_everything = (matrix_product(normalized_rows, value_projection_weight) + value_offset_bias).reshape(sequence_length, KEY_VALUE_HEADS, HEAD_SIZE)
    key_raw = low_back(key_everything[:, replica_count])
    value_copy = low(low_back(value_everything[:, replica_count]))
    queries = low(rotate(query_raw, cosine[:, None, :], sine[:, None, :]))
    key_copy = low(rotate(key_raw, cosine[:, None, :], sine[:, None, :]))
    key_heads = jnp.repeat(key_copy, QUERY_PER_SHARD, axis=1)
    value_heads = jnp.repeat(value_copy, QUERY_PER_SHARD, axis=1)
    scores = low_back(jnp.einsum('qhd,khd->hqk', queries, key_heads, precision=HIGHEST) * HEAD_SIZE ** (-0.5))
    positions = jnp.arange(sequence_length, dtype=jnp.int32)
    scores = jnp.where(allowed_keys(positions, sequence_length, prefix, valid)[None], scores, NEG_FILL)
    shifted = jnp.exp(scores - lax.optimization_barrier(jnp.max(scores, -1, keepdims=True)))
    probs_all = shifted / lax.optimization_barrier(jnp.sum(shifted, -1, keepdims=True))
    attended = low(low_back(jnp.einsum('hqk,khd->qhd', low(probs_all), value_heads, precision=HIGHEST)))
    branch_attn = low_back(matrix_product(attended.reshape(sequence_length, QUERY_HEADS * HEAD_SIZE), w_output))
    middle = states + branch_attn
    normed_two = low(norm_rows(middle, gain_ffn))
    gate_act = low_back(matrix_product(normed_two, w_gate))
    up_act = low_back(matrix_product(normed_two, w_up))
    hidden = low(gate_act * jax.nn.sigmoid(gate_act) * up_act)
    return middle + low_back(matrix_product(hidden, w_down))

def reference(states, cotangent, teacher, prefix_len, validity, w_query, key_projection_weight, value_projection_weight, w_output, w_gate, w_up, w_down, b_query, key_offset_bias, value_offset_bias, gain_attn, gain_ffn):
    params = tuple((item.astype(jnp.float32) for item in (w_query, key_projection_weight, value_projection_weight, w_output, w_gate, w_up, w_down, b_query, key_offset_bias, value_offset_bias, gain_attn, gain_ffn)))
    count_all = jnp.sum(validity).astype(jnp.float32)
    tok_scale = SEQS * LEN / count_all
    cosine, sine = tables(LEN, HEAD_SIZE)
    seq_states = states.astype(jnp.float32).reshape(SEQS, LEN, MODEL_WIDTH)
    seq_cot = cotangent.astype(jnp.float32).reshape(SEQS, LEN, MODEL_WIDTH)
    seq_teacher = teacher.astype(jnp.float32).reshape(SEQS, LEN, MODEL_WIDTH)

    def one_sequence(carry, inputs):
        grad_sums, square_sum = carry
        state_seq, cot_seq, teach_seq, valid_seq, prefix = inputs
        weight_rows = valid_seq.astype(jnp.float32)[:, None]

        def objective(layer_params, layer_in):
            result = sequence_layer(layer_params, layer_in, valid_seq, prefix, cosine, sine)
            deviation = result - teach_seq
            squares = jnp.sum(weight_rows * deviation * deviation)
            return (jnp.sum(cot_seq * result) + 0.5 * tok_scale * squares, (result, squares))
        _, pull_back, aux_pair = jax.vjp(objective, params, state_seq, has_aux=True)
        result, squares = aux_pair
        grad_params, grad_in = pull_back(jnp.ones((), jnp.float32))
        grad_sums = jax.tree.map(lambda running, update: running + update, grad_sums, grad_params)
        return ((grad_sums, square_sum + squares), (result.astype(jnp.bfloat16), grad_in))
    start = (tuple((jnp.zeros_like(item) for item in params)), jnp.zeros((), jnp.float32))
    (grad_sums, square_sum), (outs_seq, grads_seq) = lax.scan(one_sequence, start, (seq_states, seq_cot, seq_teacher, validity, prefix_len))
    distill_loss = square_sum / (2.0 * count_all * MODEL_WIDTH)
    return (outs_seq.reshape(SEQS * LEN, MODEL_WIDTH), distill_loss, grads_seq.reshape(SEQS * LEN, MODEL_WIDTH), grad_sums[0], grad_sums[1], grad_sums[2], grad_sums[3], grad_sums[4], grad_sums[5], grad_sums[6], grad_sums[7], grad_sums[8], grad_sums[9], grad_sums[10], grad_sums[11])
```

```python
import functools

import jax
import jax.numpy as jnp
from jax import lax
from jax.experimental import pallas as pl
from jax.experimental.pallas import tpu as pltpu
from jax.sharding import PartitionSpec as P

QUERY_HEADS = 12
KEY_VALUE_HEADS = 2
HEAD_SIZE = 128

NORM_EPS = 1e-06
ROPE_BASE = 10000.0
NEG_FILL = -1e30

F32 = jnp.float32
BF16 = jnp.bfloat16


def mm(spec, left, right):
    return jnp.einsum(spec, left, right, preferred_element_type=F32)


def tables(positions):
    half_width = HEAD_SIZE // 2
    inverse = ROPE_BASE ** (-(jnp.arange(half_width, dtype=F32) * 2.0 / HEAD_SIZE))
    angles = positions.astype(F32)[:, None] * inverse[None, :]
    return jnp.cos(angles), jnp.sin(angles)


def rotate(values, cosine, sine):
    half_width = values.shape[-1] // 2
    first = values[..., :half_width]
    second = values[..., half_width:]
    return jnp.concatenate(
        [first * cosine - second * sine, second * cosine + first * sine], axis=-1
    )


def after(value, *tokens):
    return lax.optimization_barrier((value,) + tokens)[0]


def swap(value, axis, size, bits):
    return lax.ppermute(value, axis, [(i, i ^ bits) for i in range(size)])


def ring_position(index, size):
    return jnp.where(index % 2 == 0, index // 2, size - (index + 1) // 2)


def ring_member(position, size):
    position = position % size
    return jnp.where(position < size // 2, 2 * position, 2 * (size - position) - 1)


def ring_pairs(size, step):
    ring = list(range(0, size, 2)) + list(range(size - 1, 0, -2))
    return [(ring[i], ring[(i + step) % size]) for i in range(size)]


class Gather:
    def __init__(self, shard, size):
        self.size = size
        self.shard = shard
        self.up = self.down = shard
        self.ups, self.downs = [], []
        self.steps = size // 2
        self.done = 0

    def step(self, *tokens):
        size, rows = self.size, self.shard.shape[0]
        up, down = self.up, self.down
        if self.done == self.steps - 1:
            up, down = up[: rows // 2], down[rows // 2 :]
        if tokens:
            up, down = lax.optimization_barrier((up, down) + tokens)[:2]
        self.up = lax.ppermute(up, "dp", ring_pairs(size, 1))
        self.down = lax.ppermute(down, "dp", ring_pairs(size, -1))
        self.ups.append(self.up)
        self.downs.append(self.down)
        self.done += 1
        return self.up, self.down

    def whole(self):
        size = self.size
        rows, cols = self.shard.shape
        mine = ring_position(lax.axis_index("dp"), size)
        count = self.steps
        from_up = [ring_member(mine - k, size) for k in range(1, count + 1)]
        from_down = [ring_member(mine + k, size) for k in range(1, count + 1)]
        where = jnp.stack([lax.axis_index("dp")] + from_up + from_down).astype(jnp.int32)
        blocks = [self.shard] + self.ups + self.downs
        spans = [(0, rows)] + ([(0, rows)] * (count - 1) + [(0, rows // 2)])
        spans += [(0, rows)] * (count - 1) + [(rows // 2, rows - rows // 2)]
        return place(blocks, spans, where, size).reshape(size * rows, cols)


def place_kernel(spans, where, *refs):
    blocks, (out, sem) = refs[: len(spans)], refs[len(spans) :]
    copies = []
    for k, (start, length) in enumerate(spans):
        copies.append(
            pltpu.make_async_copy(
                blocks[k], out.at[where[k], pl.ds(start, length)], sem.at[k]
            )
        )
    for copy in copies:
        copy.start()
    for copy in copies:
        copy.wait()


def place(blocks, spans, where, size):
    rows, cols = blocks[0].shape
    anywhere = pl.BlockSpec(memory_space=pl.ANY)
    return pl.pallas_call(
        functools.partial(place_kernel, spans),
        out_shape=jax.ShapeDtypeStruct((size, rows, cols), blocks[0].dtype),
        in_specs=[pl.BlockSpec(memory_space=pltpu.SMEM)] + [anywhere] * len(blocks),
        out_specs=anywhere,
        scratch_shapes=[pltpu.SemaphoreType.DMA((len(blocks),))],
    )(where, *blocks)


class Scatter:
    def __init__(self, blocks, size):
        self.blocks, self.size = blocks, size
        self.mine = ring_position(lax.axis_index("dp"), size)
        self.rows = blocks.shape[1]
        self.left = size // 2
        self.up = self.down = None

    def block(self, offset):
        return lax.dynamic_index_in_dim(
            self.blocks, ring_member(self.mine + offset, self.size), 0, keepdims=False
        )

    def step(self, *tokens):
        half = self.rows // 2
        if self.up is None:
            up = self.block(self.left)
            up, down = up[:half], up[half:]
        else:
            up, down = self.block(self.left), self.block(-self.left)
            if self.left == self.size // 2 - 1:
                up = jnp.concatenate([add16(up[:half], self.up), up[half:]])
                down = jnp.concatenate([down[:half], add16(down[half:], self.down)])
            else:
                up, down = add16(up, self.up), add16(down, self.down)
        if tokens:
            up, down = lax.optimization_barrier((up, down) + tokens)[:2]
        self.up = lax.ppermute(up, "dp", ring_pairs(self.size, 1))
        self.down = lax.ppermute(down, "dp", ring_pairs(self.size, -1))
        self.left -= 1
        return self.up, self.down

    def result(self):
        own = lax.dynamic_index_in_dim(self.blocks, lax.axis_index("dp"), 0, keepdims=False)
        return own.astype(F32) + self.up.astype(F32) + self.down.astype(F32)


def add16(left, right):
    return (left.astype(F32) + right.astype(F32)).astype(BF16)


def gather_rows(rows):
    across = swap(rows, "tensor", 4, 2)
    beside = swap(rows, "tensor", 4, 1)
    corner = swap(across, "tensor", 4, 1)
    return jnp.concatenate([rows, beside, across, corner], 0)


def scatter_rows(far, near):
    rows = far.shape[0] // 2
    far_in = swap(far[rows:], "tensor", 4, 1)
    far_sum = add16(far[:rows], far_in)
    across = swap(far_sum, "tensor", 4, 2)
    near_in = swap(near[rows:], "tensor", 4, 1)
    return near[:rows].astype(F32) + near_in.astype(F32) + across.astype(F32)


def gather_small(vector, size):
    block = vector[None]
    for bit in (1, 2):
        block = jnp.concatenate([block, swap(block, "tensor", 4, bit)], 0)
    bit = 1
    while bit < size:
        block = jnp.concatenate([block, swap(block, "dp", size, bit)], 0)
        bit *= 2
    me = lax.axis_index("dp") * 4 + lax.axis_index("tensor")
    order = jnp.arange(size * 4, dtype=jnp.int32) ^ me
    return jnp.take(block, order, axis=0)


def sum_small(block, size):
    for bit in (1, 2):
        block = block + swap(block, "tensor", 4, bit)
    bit = 1
    while bit < size:
        block = block + swap(block, "dp", size, bit)
        bit *= 2
    return block


def attend(queries, keys, values, allowed, scale):
    outs, saved = [], []
    for low, high in ((0, 512), (512, 1024)):
        scores = mm("qhd,kd->hqk", queries[low:high], keys) * scale
        scores = jnp.where(allowed[None, low:high], scores, NEG_FILL)
        row_max = jnp.max(scores, -1, keepdims=True)
        shifted = jnp.exp(scores - row_max)
        row_sum = jnp.sum(shifted, -1, keepdims=True)
        low_probs = (shifted / row_sum).astype(BF16)
        outs.append(mm("hqk,kd->qhd", low_probs, values).astype(BF16))
        saved.append((row_max, row_sum))
    return jnp.concatenate(outs, 0), saved


def attend_back(queries, keys, values, grads, allowed, scale, saved):
    grad_queries, grad_keys, grad_values = [], 0.0, 0.0
    for (low, high), (row_max, row_sum) in zip(((0, 512), (512, 1024)), saved):
        query, grad = queries[low:high], grads[low:high]
        scores = mm("qhd,kd->hqk", query, keys) * scale
        scores = jnp.where(allowed[None, low:high], scores, NEG_FILL)
        probs = jnp.exp(scores - row_max) / row_sum
        grad_probs = mm("qhd,kd->hqk", grad, values)
        spread = jnp.sum(probs * grad_probs, -1, keepdims=True)
        grad_scores = (probs * (grad_probs - spread)).astype(BF16)
        grad_queries.append(mm("hqk,kd->qhd", grad_scores, keys) * scale)
        grad_keys = grad_keys + mm("hqk,qhd->kd", grad_scores, query) * scale
        grad_values = grad_values + mm("hqk,qhd->kd", probs.astype(BF16), grad)
    return jnp.concatenate(grad_queries, 0), grad_keys, grad_values


def body(
    states,
    cotangent,
    teacher,
    prefix_len,
    validity,
    w_query,
    key_projection_weight,
    value_projection_weight,
    w_output,
    w_gate,
    w_up,
    w_down,
    b_query,
    key_offset_bias,
    value_offset_bias,
    gain_attn,
    gain_ffn,
):
    groups = lax.axis_size("tensor")
    dp_size = lax.axis_size("dp")
    tensor_index = lax.axis_index("tensor")
    dp_index = lax.axis_index("dp")
    row_count, feature_count = states.shape
    all_rows = row_count * groups
    local_heads = QUERY_HEADS // groups
    head_cols = local_heads * HEAD_SIZE
    kv_head = tensor_index * local_heads // (QUERY_HEADS // KEY_VALUE_HEADS)
    score_scale = HEAD_SIZE ** (-0.5)
    shard_rows = w_query.shape[0]

    blocks = [tensor_index ^ r for r in range(groups)]
    positions = jnp.concatenate(
        [b * row_count + jnp.arange(row_count, dtype=jnp.int32) for b in blocks]
    )
    valid_seq = validity.reshape(groups, row_count)
    valid_all = jnp.concatenate(
        [lax.dynamic_index_in_dim(valid_seq, b, 0, keepdims=False) for b in blocks]
    )
    valid_rows = valid_all[:row_count].astype(F32)[:, None]

    bias_part, kv_part = b_query.shape[0], key_offset_bias.shape[0]
    seq_count = jnp.sum(validity).astype(F32)[None]
    small = jnp.concatenate(
        [
            b_query.astype(F32),
            gain_attn.astype(F32),
            gain_ffn.astype(F32),
            key_offset_bias.astype(F32),
            value_offset_bias.astype(F32),
            seq_count,
        ]
    )
    small = gather_small(small, dp_size)
    at = 0
    pieces = []
    for width in (bias_part, bias_part, bias_part, kv_part, kv_part, 1):
        pieces.append(small[:, at : at + width].reshape(-1))
        at += width
    bias_query, gain_one, gain_two, bias_key, bias_value, counts = pieces
    count_all = jnp.sum(counts) / groups
    query_bias = lax.dynamic_slice_in_dim(bias_query, tensor_index * head_cols, head_cols, 0)
    key_bias = lax.dynamic_slice_in_dim(bias_key, kv_head * HEAD_SIZE, HEAD_SIZE, 0)
    value_bias = lax.dynamic_slice_in_dim(bias_value, kv_head * HEAD_SIZE, HEAD_SIZE, 0)
    qkv_bias = jnp.concatenate([query_bias, key_bias, value_bias])

    kv = jnp.concatenate(
        [
            key_projection_weight.reshape(-1, KEY_VALUE_HEADS, HEAD_SIZE),
            value_projection_weight.reshape(-1, KEY_VALUE_HEADS, HEAD_SIZE),
        ],
        -1,
    )
    kv_own = lax.dynamic_index_in_dim(kv, kv_head, 1, keepdims=False)
    kv_other = lax.dynamic_index_in_dim(kv, 1 - kv_head, 1, keepdims=False)
    kv_pair = jnp.stack([kv_own, swap(kv_other, "tensor", 4, 2)])
    kv_beside = swap(kv_pair, "tensor", 4, 1)
    kv_rel = jnp.stack([kv_pair[0], kv_beside[0], kv_pair[1], kv_beside[1]])
    kv_rows = jnp.take(kv_rel, jnp.arange(groups, dtype=jnp.int32) ^ tensor_index, axis=0)
    kv_rows = kv_rows.reshape(shard_rows, 2 * HEAD_SIZE)

    states_all = gather_rows(states)
    ring_q = Gather(w_query, dp_size)
    ring_kv = Gather(kv_rows, dp_size)
    ring_o = Gather(w_output.T, dp_size)
    ring_gate = Gather(w_gate, dp_size)
    ring_up = Gather(w_up, dp_size)
    ring_down = Gather(w_down.T, dp_size)
    window = []

    def go(ring, steps):
        for _ in range(steps):
            tokens = window[-2] if len(window) >= 2 else ()
            window.append(ring.step(*tokens))

    steps = dp_size // 2
    for _ in range(steps):
        ring_q.step()
        ring_kv.step()
        ring_o.step()
    window.append(ring_q.ups[-2:-1])
    for _ in range(steps):
        go(ring_gate, 1)
        go(ring_up, 1)
    go(ring_down, steps)

    states_f = states_all.astype(F32)
    rms_one = lax.rsqrt(jnp.mean(states_f * states_f, -1, keepdims=True) + NORM_EPS)
    normed_all = (states_f * rms_one * gain_one).astype(BF16)
    w_qkv = jnp.concatenate([ring_q.whole(), ring_kv.whole()], 1)
    qkv = jnp.dot(normed_all, w_qkv, preferred_element_type=F32) + qkv_bias
    cosine, sine = tables(positions)
    queries = rotate(
        qkv[:, :head_cols].reshape(all_rows, local_heads, HEAD_SIZE),
        cosine[:, None, :],
        sine[:, None, :],
    ).astype(BF16)
    keys = rotate(qkv[:, head_cols : head_cols + HEAD_SIZE], cosine, sine).astype(BF16)
    values = qkv[:, head_cols + HEAD_SIZE :].astype(BF16)
    allowed = (positions[None, :] <= positions[:, None]) | (positions[None, :] < prefix_len[0])
    allowed = allowed & (valid_all[None, :] > 0)
    attended, saved = attend(queries, keys, values, allowed, score_scale)
    attended = attended.reshape(all_rows, head_cols)
    output_t = ring_o.whole()
    half = all_rows // 2
    far = mm("rh,dh->rd", attended[half:], output_t).astype(BF16)
    near = mm("rh,dh->rd", attended[:half], output_t).astype(BF16)
    states_own = states_f[:row_count]
    middle = states_own + scatter_rows(far, near)

    rms_two = lax.rsqrt(jnp.mean(middle * middle, -1, keepdims=True) + NORM_EPS)
    normed_two = (middle * rms_two * gain_two).astype(BF16)
    normed_two_all = gather_rows(normed_two)
    gate_w, up_w = ring_gate.whole(), ring_up.whole()
    gate_act = jnp.dot(normed_two_all, gate_w, preferred_element_type=F32)
    up_act = jnp.dot(normed_two_all, up_w, preferred_element_type=F32)
    sigma = jax.nn.sigmoid(gate_act)
    hidden = (gate_act * sigma * up_act).astype(BF16)
    down_t = ring_down.whole()
    far = mm("rf,df->rd", hidden[half:], down_t).astype(BF16)
    near = mm("rf,df->rd", hidden[:half], down_t).astype(BF16)
    result = middle + scatter_rows(far, near)

    deviation = result - teacher.astype(F32)
    square_sum = jnp.sum(valid_rows * deviation * deviation)
    token_total = float(all_rows * dp_size)
    grad_result = cotangent.astype(F32) + token_total / count_all * valid_rows * deviation

    grad_two_all = gather_rows(grad_result.astype(BF16))

    def split(gradient):
        return gradient.astype(BF16).reshape(dp_size, shard_rows, -1)

    grad_down = mm("rd,rf->df", grad_two_all, hidden)
    sum_down = Scatter(split(grad_down), dp_size)
    grad_hidden = mm("rd,df->rf", grad_two_all, down_t)
    grad_gate_act = (grad_hidden * up_act * sigma * (1.0 + gate_act * (1.0 - sigma))).astype(BF16)
    grad_up_act = (grad_hidden * gate_act * sigma).astype(BF16)
    sum_gate = Scatter(split(mm("rd,rf->df", normed_two_all, grad_gate_act)), dp_size)
    sum_up = Scatter(split(mm("rd,rf->df", normed_two_all, grad_up_act)), dp_size)
    far = mm("rf,df->rd", grad_gate_act[half:], gate_w)
    far = (far + mm("rf,df->rd", grad_up_act[half:], up_w)).astype(BF16)
    near = mm("rf,df->rd", grad_gate_act[:half], gate_w)
    near = (near + mm("rf,df->rd", grad_up_act[:half], up_w)).astype(BF16)
    grad_normed_two = scatter_rows(far, near)
    scaled_two = middle * rms_two
    grad_gain_two = jnp.sum(grad_normed_two * scaled_two, 0)
    pulled = gain_two * grad_normed_two
    grad_middle = grad_result + rms_two * (
        pulled - scaled_two * jnp.mean(pulled * scaled_two, -1, keepdims=True)
    )
    grad_one_all = gather_rows(grad_middle.astype(BF16))
    sum_o = Scatter(split(mm("rd,rh->dh", grad_one_all, attended)), dp_size)
    grad_attended = mm("rd,dh->rh", grad_one_all, output_t).astype(BF16)
    grad_queries, grad_keys, grad_values = attend_back(
        queries,
        keys,
        values,
        grad_attended.reshape(all_rows, local_heads, HEAD_SIZE),
        allowed,
        score_scale,
        saved,
    )
    grad_query_raw = rotate(grad_queries, cosine[:, None, :], -sine[:, None, :]).astype(BF16)
    grad_key_raw = rotate(grad_keys, cosine, -sine).astype(BF16)
    grad_qkv = jnp.concatenate(
        [grad_query_raw.reshape(all_rows, head_cols), grad_key_raw, grad_values.astype(BF16)], 1
    )
    sum_qkv = Scatter(split(mm("rd,rf->df", normed_all, grad_qkv)), dp_size)
    grad_qkv_bias = jnp.sum(grad_qkv.astype(F32), 0)
    grad_normed_part = mm("rf,df->rd", grad_qkv, w_qkv)
    scaled_one = states_f * rms_one
    grad_gain_one = jnp.sum(grad_normed_part * scaled_one, 0)
    grad_normed_part = grad_normed_part.astype(BF16)
    grad_normed = scatter_rows(grad_normed_part[half:], grad_normed_part[:half])
    pulled = gain_one * grad_normed
    scaled_own = scaled_one[:row_count]
    grad_states = grad_middle + rms_one[:row_count] * (
        pulled - scaled_own * jnp.mean(pulled * scaled_own, -1, keepdims=True)
    )

    window.clear()

    def send(ring, steps):
        for _ in range(steps):
            tokens = window[-2] if len(window) >= 2 else ()
            window.append(ring.step(*tokens))

    send(sum_down, 1)
    send(sum_down, 1)
    for _ in range(steps - 2):
        send(sum_down, 1)
        send(sum_gate, 1)
    send(sum_gate, 1)
    send(sum_up, 1)
    send(sum_gate, 1)
    send(sum_up, 1)
    for _ in range(steps - 2):
        send(sum_up, 1)
        send(sum_o, 1)
    for _ in range(2):
        sum_o.step()
    for _ in range(steps):
        sum_qkv.step()

    qkv_sum = sum_qkv.result()
    grad_w_query = qkv_sum[:, :head_cols]
    kv_sum = qkv_sum[:, head_cols:].reshape(groups, shard_rows // groups, 2 * HEAD_SIZE)
    kv_rel = [lax.dynamic_index_in_dim(kv_sum, b, 0, keepdims=False) for b in blocks]
    kv_in = swap(jnp.stack([kv_rel[1], kv_rel[3]]), "tensor", 4, 1)
    kv_own = kv_rel[0] + kv_in[0]
    kv_other = swap(kv_rel[2] + kv_in[1], "tensor", 4, 2)
    first = kv_head == 0
    kv_low = jnp.where(first, kv_own, kv_other)
    kv_high = jnp.where(first, kv_other, kv_own)
    grad_w_key = jnp.concatenate([kv_low[:, :HEAD_SIZE], kv_high[:, :HEAD_SIZE]], 1)
    grad_w_value = jnp.concatenate([kv_low[:, HEAD_SIZE:], kv_high[:, HEAD_SIZE:]], 1)

    def put(length, vector, index):
        return lax.dynamic_update_slice_in_dim(jnp.zeros((length,), F32), vector, index, 0)

    kv_cols = KEY_VALUE_HEADS * HEAD_SIZE
    packed = jnp.concatenate(
        [
            put(QUERY_HEADS * HEAD_SIZE, grad_qkv_bias[:head_cols], tensor_index * head_cols),
            put(kv_cols, grad_qkv_bias[head_cols : head_cols + HEAD_SIZE], kv_head * HEAD_SIZE),
            put(kv_cols, grad_qkv_bias[head_cols + HEAD_SIZE :], kv_head * HEAD_SIZE),
            grad_gain_one,
            grad_gain_two,
            jnp.full((HEAD_SIZE,), square_sum, F32),
        ]
    )
    packed = sum_small(packed.reshape(-1, HEAD_SIZE), dp_size).reshape(-1)
    device = dp_index * groups + tensor_index
    smalls = []
    at = 0
    for width in (bias_part, kv_part, kv_part, bias_part, bias_part):
        smalls.append(lax.dynamic_slice_in_dim(packed, at + device * width, width, 0))
        at += width * dp_size * groups
    distill_loss = packed[at] / (2.0 * count_all * feature_count)
    return (
        result.astype(BF16),
        distill_loss,
        grad_states,
        grad_w_query,
        grad_w_key,
        grad_w_value,
        sum_o.result().T,
        sum_gate.result(),
        sum_up.result(),
        sum_down.result().T,
        smalls[0],
        smalls[1],
        smalls[2],
        smalls[3],
        smalls[4],
    )


def solution(mesh):
    rows = P(("dp", "tensor"), None)
    flat = P(("dp", "tensor"))
    return jax.shard_map(
        body,
        mesh=mesh,
        in_specs=(
            rows,
            rows,
            rows,
            P("dp"),
            P("dp", None),
            P("dp", "tensor"),
            rows,
            rows,
            P("tensor", "dp"),
            P("dp", "tensor"),
            P("dp", "tensor"),
            P("tensor", "dp"),
            flat,
            flat,
            flat,
            flat,
            flat,
        ),
        out_specs=(
            rows,
            P(),
            rows,
            P("dp", "tensor"),
            rows,
            rows,
            P("tensor", "dp"),
            P("dp", "tensor"),
            P("dp", "tensor"),
            P("tensor", "dp"),
            flat,
            flat,
            flat,
            flat,
            flat,
        ),
        check_vma=False,
    )
```

```python
import functools

import jax
import jax.numpy as jnp
from jax import lax
from jax.experimental import pallas as pl
from jax.experimental.pallas import tpu as pltpu
from jax.experimental.layout import Layout, with_layout_constraint
from jax.sharding import PartitionSpec as P

QUERY_HEADS = 12
KEY_VALUE_HEADS = 2
HEAD_SIZE = 128

NORM_EPS = 1e-06
ROPE_BASE = 10000.0
NEG_FILL = -1e30

F32 = jnp.float32
BF16 = jnp.bfloat16


def mm(spec, left, right):
    return jnp.einsum(spec, left, right, preferred_element_type=F32)


def tables(positions):
    half_width = HEAD_SIZE // 2
    inverse = ROPE_BASE ** (-(jnp.arange(half_width, dtype=F32) * 2.0 / HEAD_SIZE))
    angles = positions.astype(F32)[:, None] * inverse[None, :]
    return jnp.cos(angles), jnp.sin(angles)


def rotate(values, cosine, sine):
    half_width = values.shape[-1] // 2
    first = values[..., :half_width]
    second = values[..., half_width:]
    return jnp.concatenate(
        [first * cosine - second * sine, second * cosine + first * sine], axis=-1
    )


def after(value, *tokens):
    return lax.optimization_barrier((value,) + tokens)[0]


class Line:
    def __init__(self):
        self.last = ()

    def hold(self, *values):
        if self.last:
            values = lax.optimization_barrier(tuple(values) + tuple(self.last))[: len(values)]
        return values if len(values) > 1 else values[0]

    def mark(self, *tokens):
        self.last = tokens

    def pass_by(self, *values):
        values = self.hold(*values)
        self.last = values if isinstance(values, tuple) else (values,)
        return values


def swap(value, axis, size, bits):
    return lax.ppermute(value, axis, [(i, i ^ bits) for i in range(size)])


def ring_position(index, size):
    return jnp.where(index % 2 == 0, index // 2, size - (index + 1) // 2)


def ring_member(position, size):
    position = position % size
    return jnp.where(position < size // 2, 2 * position, 2 * (size - position) - 1)


def ring_pairs(size, step):
    ring = list(range(0, size, 2)) + list(range(size - 1, 0, -2))
    return [(ring[i], ring[(i + step) % size]) for i in range(size)]


class Gather:
    def __init__(self, shard, size):
        self.size = size
        self.shard = shard
        self.up = self.down = shard
        self.ups, self.downs = [], []
        self.steps = size // 2
        self.done = 0

    def step(self, line):
        size, rows = self.size, self.shard.shape[0]
        up, down = self.up, self.down
        if self.done == self.steps - 1:
            up, down = up[: rows // 2], down[rows // 2 :]
        up, down = line.pass_by(up, down)
        self.up = lax.ppermute(up, "dp", ring_pairs(size, 1))
        self.down = lax.ppermute(down, "dp", ring_pairs(size, -1))
        self.ups.append(self.up)
        self.downs.append(self.down)
        self.done += 1
        return self.up, self.down

    def whole(self):
        size = self.size
        rows, cols = self.shard.shape
        mine = ring_position(lax.axis_index("dp"), size)
        count = self.steps
        from_up = [ring_member(mine - k, size) for k in range(1, count + 1)]
        from_down = [ring_member(mine + k, size) for k in range(1, count + 1)]
        where = jnp.stack([lax.axis_index("dp")] + from_up + from_down).astype(jnp.int32)
        blocks = [self.shard] + self.ups + self.downs
        spans = [(0, rows)] + ([(0, rows)] * (count - 1) + [(0, rows // 2)])
        spans += [(0, rows)] * (count - 1) + [(rows // 2, rows - rows // 2)]
        return place(blocks, spans, where, size).reshape(size * rows, cols)


def place_kernel(spans, where, *refs):
    count = len(spans)
    blocks, out = refs[:count], refs[count]
    held, sem_in, sem_out = refs[count + 1 :]
    loads, stores = [], []
    for k, (start, length) in enumerate(spans):
        part = held.at[k, pl.ds(0, length)]
        loads.append(pltpu.make_async_copy(blocks[k], part, sem_in.at[k]))
        target = out.at[where[k], pl.ds(start, length)]
        stores.append(pltpu.make_async_copy(part, target, sem_out.at[k]))
    for copy in loads:
        copy.start()
    for load, store in zip(loads, stores):
        load.wait()
        store.start()
    for copy in stores:
        copy.wait()


def place(blocks, spans, where, size):
    rows, cols = blocks[0].shape
    count = len(blocks)
    anywhere = pl.BlockSpec(memory_space=pl.ANY)
    return pl.pallas_call(
        functools.partial(place_kernel, spans),
        out_shape=jax.ShapeDtypeStruct((size, rows, cols), blocks[0].dtype),
        in_specs=[pl.BlockSpec(memory_space=pltpu.SMEM)] + [anywhere] * count,
        out_specs=anywhere,
        scratch_shapes=[
            pltpu.VMEM((count, rows, cols), blocks[0].dtype),
            pltpu.SemaphoreType.DMA((count,)),
            pltpu.SemaphoreType.DMA((count,)),
        ],
    )(where, *blocks)


class Scatter:
    def __init__(self, blocks, size):
        self.blocks, self.size = blocks, size
        self.mine = ring_position(lax.axis_index("dp"), size)
        self.rows = blocks.shape[1]
        self.left = size // 2
        self.up = self.down = None

    def block(self, offset):
        return lax.dynamic_index_in_dim(
            self.blocks, ring_member(self.mine + offset, self.size), 0, keepdims=False
        )

    def step(self, line):
        half = self.rows // 2
        if self.up is None:
            up = self.block(self.left)
            up, down = up[:half], up[half:]
        else:
            up, down = self.block(self.left), self.block(-self.left)
            if self.left == self.size // 2 - 1:
                up = jnp.concatenate([add16(up[:half], self.up), up[half:]])
                down = jnp.concatenate([down[:half], add16(down[half:], self.down)])
            else:
                up, down = add16(up, self.up), add16(down, self.down)
        up, down = line.pass_by(up, down)
        self.up = lax.ppermute(up, "dp", ring_pairs(self.size, 1))
        self.down = lax.ppermute(down, "dp", ring_pairs(self.size, -1))
        self.left -= 1
        return self.up, self.down

    def result(self):
        own = lax.dynamic_index_in_dim(self.blocks, lax.axis_index("dp"), 0, keepdims=False)
        return own.astype(F32) + self.up.astype(F32) + self.down.astype(F32)


def add16(left, right):
    return (left.astype(F32) + right.astype(F32)).astype(BF16)


class Rows:
    def __init__(self, rows, line):
        self.rows = line.pass_by(rows)
        self.across = swap(self.rows, "tensor", 4, 2)
        self.beside = swap(self.rows, "tensor", 4, 1)

    def turn(self, line):
        self.across = line.pass_by(self.across)
        self.corner = swap(self.across, "tensor", 4, 1)

    def whole(self):
        return jnp.concatenate([self.rows, self.beside, self.across, self.corner], 0)


class Sum:
    def far(self, far, line):
        rows = far.shape[0] // 2
        self.far_own, far = far[:rows], line.pass_by(far[rows:])
        self.far_in = swap(far, "tensor", 4, 1)

    def turn(self, line):
        self.across = swap(line.pass_by(add16(self.far_own, self.far_in)), "tensor", 4, 2)

    def near(self, near, line):
        rows = near.shape[0] // 2
        self.near_own, near = near[:rows], line.pass_by(near[rows:])
        self.near_in = swap(near, "tensor", 4, 1)

    def result(self):
        total = self.near_own.astype(F32) + self.near_in.astype(F32)
        return total + self.across.astype(F32)


def gather_small(vector, size):
    block = vector[None]
    for bit in (1, 2):
        block = jnp.concatenate([block, swap(block, "tensor", 4, bit)], 0)
    bit = 1
    while bit < size:
        block = jnp.concatenate([block, swap(block, "dp", size, bit)], 0)
        bit *= 2
    me = lax.axis_index("dp") * 4 + lax.axis_index("tensor")
    order = jnp.arange(size * 4, dtype=jnp.int32) ^ me
    return jnp.take(block, order, axis=0)


def sum_small(block, size):
    for bit in (1, 2):
        block = block + swap(block, "tensor", 4, bit)
    bit = 1
    while bit < size:
        block = block + swap(block, "dp", size, bit)
        bit *= 2
    return block


def attend(queries, keys, values, allowed, scale):
    scores = mm("qhd,kd->hqk", queries, keys) * scale
    scores = jnp.where(allowed[None], scores, NEG_FILL)
    row_max = jnp.max(scores, -1, keepdims=True)
    shifted = jnp.exp(scores - row_max)
    row_sum = jnp.sum(shifted, -1, keepdims=True)
    low_probs = (shifted / row_sum).astype(BF16)
    out = mm("hqk,kd->qhd", low_probs, values).astype(BF16)
    return out.reshape(queries.shape[0], -1), (row_max, row_sum)


def attend_back(query, keys, values, grad, allowed, scale, saved):
    row_max, row_sum = saved
    scores = mm("qhd,kd->hqk", query, keys) * scale
    scores = jnp.where(allowed[None], scores, NEG_FILL)
    probs = jnp.exp(scores - row_max) / row_sum
    grad_probs = mm("qhd,kd->hqk", grad, values)
    spread = jnp.sum(probs * grad_probs, -1, keepdims=True)
    grad_scores = (probs * (grad_probs - spread)).astype(BF16)
    grad_query = mm("hqk,kd->qhd", grad_scores, keys) * scale
    grad_keys = mm("hqk,qhd->kd", grad_scores, query) * scale
    grad_values = mm("hqk,qhd->kd", probs.astype(BF16), grad)
    return grad_query, grad_keys, grad_values


def body(
    states,
    cotangent,
    teacher,
    prefix_len,
    validity,
    w_query,
    key_projection_weight,
    value_projection_weight,
    w_output,
    w_gate,
    w_up,
    w_down,
    b_query,
    key_offset_bias,
    value_offset_bias,
    gain_attn,
    gain_ffn,
):
    groups = lax.axis_size("tensor")
    dp_size = lax.axis_size("dp")
    tensor_index = lax.axis_index("tensor")
    dp_index = lax.axis_index("dp")
    row_count, feature_count = states.shape
    all_rows = row_count * groups
    local_heads = QUERY_HEADS // groups
    head_cols = local_heads * HEAD_SIZE
    kv_head = tensor_index * local_heads // (QUERY_HEADS // KEY_VALUE_HEADS)
    score_scale = HEAD_SIZE ** (-0.5)
    shard_rows = w_query.shape[0]

    blocks = [tensor_index ^ r for r in range(groups)]
    positions = jnp.concatenate(
        [b * row_count + jnp.arange(row_count, dtype=jnp.int32) for b in blocks]
    )
    valid_seq = validity.reshape(groups, row_count)
    valid_all = jnp.concatenate(
        [lax.dynamic_index_in_dim(valid_seq, b, 0, keepdims=False) for b in blocks]
    )
    valid_rows = valid_all[:row_count].astype(F32)[:, None]

    bias_part, kv_part = b_query.shape[0], key_offset_bias.shape[0]
    seq_count = jnp.sum(validity).astype(F32)[None]
    small = jnp.concatenate(
        [
            b_query.astype(F32),
            gain_attn.astype(F32),
            gain_ffn.astype(F32),
            key_offset_bias.astype(F32),
            value_offset_bias.astype(F32),
            seq_count,
        ]
    )
    small = gather_small(small, dp_size)
    at = 0
    pieces = []
    for width in (bias_part, bias_part, bias_part, kv_part, kv_part, 1):
        pieces.append(small[:, at : at + width].reshape(-1))
        at += width
    bias_query, gain_one, gain_two, bias_key, bias_value, counts = pieces
    count_all = jnp.sum(counts) / groups
    query_bias = lax.dynamic_slice_in_dim(bias_query, tensor_index * head_cols, head_cols, 0)
    key_bias = lax.dynamic_slice_in_dim(bias_key, kv_head * HEAD_SIZE, HEAD_SIZE, 0)
    value_bias = lax.dynamic_slice_in_dim(bias_value, kv_head * HEAD_SIZE, HEAD_SIZE, 0)
    qkv_bias = jnp.concatenate([query_bias, key_bias, value_bias])

    kv = jnp.concatenate(
        [
            key_projection_weight.reshape(-1, KEY_VALUE_HEADS, HEAD_SIZE),
            value_projection_weight.reshape(-1, KEY_VALUE_HEADS, HEAD_SIZE),
        ],
        -1,
    )
    kv_own = lax.dynamic_index_in_dim(kv, kv_head, 1, keepdims=False)
    kv_other = lax.dynamic_index_in_dim(kv, 1 - kv_head, 1, keepdims=False)
    kv_pair = jnp.stack([kv_own, swap(kv_other, "tensor", 4, 2)])
    kv_beside = swap(kv_pair, "tensor", 4, 1)
    kv_rel = jnp.stack([kv_pair[0], kv_beside[0], kv_pair[1], kv_beside[1]])
    kv_rows = jnp.take(kv_rel, jnp.arange(groups, dtype=jnp.int32) ^ tensor_index, axis=0)
    kv_rows = kv_rows.reshape(shard_rows, 2 * HEAD_SIZE)

    steps = dp_size // 2
    line = Line()
    ring_gate = Gather(w_gate, dp_size)
    ring_up = Gather(w_up, dp_size)
    ring_down = Gather(w_down.T, dp_size)
    ring_att = Gather(jnp.concatenate([w_query, kv_rows, w_output.T], 1), dp_size)
    rows_one = Rows(states, line)
    for _ in range(steps - 1):
        ring_att.step(line)
    rows_one.turn(line)
    ring_att.step(line)
    queue = [ring_gate, ring_up] * (steps - 1) + [ring_down, ring_gate, ring_up]
    queue += [ring_down] * (steps - 1)

    def send(count):
        for _ in range(count):
            queue.pop(0).step(line)

    send(2 * (steps - 3))

    half = all_rows // 2
    states_f = rows_one.whole().astype(F32)
    rms_one = lax.rsqrt(jnp.mean(states_f * states_f, -1, keepdims=True) + NORM_EPS)
    normed_all = (states_f * rms_one * gain_one).astype(BF16)
    w_att = ring_att.whole()
    qkv_cols = head_cols + 2 * HEAD_SIZE
    w_qkv, output_t = w_att[:, :qkv_cols], w_att[:, qkv_cols:]
    qkv = jnp.dot(line.hold(normed_all), w_qkv, preferred_element_type=F32) + qkv_bias
    line.mark(qkv)
    send(1)
    cosine, sine = tables(positions)
    queries = rotate(
        qkv[:, :head_cols].reshape(all_rows, local_heads, HEAD_SIZE),
        cosine[:, None, :],
        sine[:, None, :],
    ).astype(BF16)
    keys = rotate(qkv[:, head_cols : head_cols + HEAD_SIZE], cosine, sine).astype(BF16)
    values = qkv[:, head_cols + HEAD_SIZE :].astype(BF16)
    allowed = (positions[None, :] <= positions[:, None]) | (positions[None, :] < prefix_len[0])
    allowed = allowed & (valid_all[None, :] > 0)
    sum_one = Sum()
    attended_far, saved_far = attend(
        line.hold(queries[half:]), keys, values, allowed[half:], score_scale
    )
    far = mm("rh,dh->rd", attended_far, output_t).astype(BF16)
    line.mark(far)
    sum_one.far(far, line)
    send(1)
    attended_near, saved_near = attend(
        line.hold(queries[:half]), keys, values, allowed[:half], score_scale
    )
    line.mark(attended_near)
    sum_one.turn(line)
    near = mm("rh,dh->rd", line.hold(attended_near), output_t).astype(BF16)
    sum_one.near(near, line)
    send(1)
    states_own = states_f[:row_count]
    middle = states_own + sum_one.result()

    rms_two = lax.rsqrt(jnp.mean(middle * middle, -1, keepdims=True) + NORM_EPS)
    normed_two = (middle * rms_two * gain_two).astype(BF16)
    rows_two = Rows(normed_two, line)
    send(2)
    rows_two.turn(line)
    send(2)
    normed_two_all = rows_two.whole()
    gate_w, up_w = ring_gate.whole(), ring_up.whole()
    gate_act = jnp.dot(line.hold(normed_two_all), gate_w, preferred_element_type=F32)
    line.mark(gate_act)
    send(1)
    up_act = jnp.dot(line.hold(normed_two_all), up_w, preferred_element_type=F32)
    sigma = jax.nn.sigmoid(gate_act)
    hidden = (gate_act * sigma * up_act).astype(BF16)
    line.mark(hidden)
    send(len(queue))
    down_t = ring_down.whole()
    sum_two = Sum()
    far = mm("rf,df->rd", hidden[half:], down_t).astype(BF16)
    line.mark(far)
    sum_two.far(far, line)
    near = mm("rf,df->rd", line.hold(hidden[:half]), down_t).astype(BF16)
    line.mark(near)
    sum_two.turn(line)
    sum_two.near(near, line)
    result = middle + sum_two.result()

    deviation = result - teacher.astype(F32)
    square_sum = jnp.sum(valid_rows * deviation * deviation)
    token_total = float(all_rows * dp_size)
    grad_result = cotangent.astype(F32) + token_total / count_all * valid_rows * deviation

    rows_back = Rows(grad_result.astype(BF16), line)

    def weight_grad(left, right):
        product = mm("rd,rf->df", left, right).astype(BF16)
        return with_layout_constraint(product, Layout(major_to_minor=(0, 1)))

    def split(gradient):
        return gradient.reshape(dp_size, shard_rows, -1)

    def gate_back(grads, part):
        grad_hidden = mm("rd,df->rf", grads, down_t)
        gate, up, sig = gate_act[part], up_act[part], sigma[part]
        grad_gate = grad_hidden * up * sig * (1.0 + gate * (1.0 - sig))
        grad_up = grad_hidden * gate * sig
        return grad_gate.astype(BF16), grad_up.astype(BF16)

    def normed_back(gate_grads, up_grads):
        total = mm("rf,df->rd", gate_grads, gate_w) + mm("rf,df->rd", up_grads, up_w)
        return total.astype(BF16)

    near_part, far_part = slice(0, half), slice(half, all_rows)
    near_grads = jnp.concatenate([rows_back.rows, line.hold(rows_back.beside)], 0)
    gate_near, up_near = gate_back(near_grads, near_part)
    line.mark(gate_near, up_near)
    rows_back.turn(line)
    grad_two_all = rows_back.whole()
    grad_down = weight_grad(line.hold(grad_two_all), hidden)
    line.mark(grad_down)
    sum_down = Scatter(split(grad_down), dp_size)
    sum_down.step(line)
    gate_far, up_far = gate_back(line.hold(grad_two_all[half:]), far_part)
    line.mark(gate_far, up_far)
    sum_down.step(line)
    sum_back = Sum()
    far = normed_back(line.hold(gate_far), up_far)
    line.mark(far)
    sum_back.far(far, line)
    grad_gate = weight_grad(
        line.hold(normed_two_all), jnp.concatenate([gate_near, gate_far], 0)
    )
    line.mark(grad_gate)
    sum_gate = Scatter(split(grad_gate), dp_size)
    sum_back.turn(line)
    for _ in range(steps - 3):
        sum_down.step(line)
    sum_gate.step(line)
    near = normed_back(line.hold(gate_near), up_near)
    line.mark(near)
    sum_back.near(near, line)
    grad_up = weight_grad(line.hold(normed_two_all), jnp.concatenate([up_near, up_far], 0))
    line.mark(grad_up)
    sum_up = Scatter(split(grad_up), dp_size)
    sum_up.step(line)
    sum_down.step(line)
    grad_normed_two = sum_back.result()
    scaled_two = middle * rms_two
    grad_gain_two = jnp.sum(grad_normed_two * scaled_two, 0)
    pulled = gain_two * grad_normed_two
    grad_middle = grad_result + rms_two * (
        pulled - scaled_two * jnp.mean(pulled * scaled_two, -1, keepdims=True)
    )
    rows_mid = Rows(grad_middle.astype(BF16), line)
    for _ in range(steps - 3):
        sum_gate.step(line)
    rows_mid.turn(line)
    for _ in range(steps - 3):
        sum_up.step(line)
    grad_one_all = line.hold(rows_mid.whole())
    grad_attended = mm("rd,dh->rh", grad_one_all, output_t).astype(BF16)
    grad_attended = grad_attended.reshape(all_rows, local_heads, HEAD_SIZE)

    def back(part, saved):
        return attend_back(
            line.hold(queries[part]),
            keys,
            values,
            grad_attended[part],
            allowed[part],
            score_scale,
            saved,
        )

    back_far = back(far_part, saved_far)
    line.mark(*back_far)
    sum_gate.step(line)
    back_near = back(near_part, saved_near)
    line.mark(*back_near)
    grad_queries = jnp.concatenate([back_near[0], back_far[0]], 0)
    grad_keys, grad_values = back_near[1] + back_far[1], back_near[2] + back_far[2]
    grad_query_raw = rotate(grad_queries, cosine[:, None, :], -sine[:, None, :]).astype(BF16)
    grad_key_raw = rotate(grad_keys, cosine, -sine).astype(BF16)
    grad_qkv = jnp.concatenate(
        [grad_query_raw.reshape(all_rows, head_cols), grad_key_raw, grad_values.astype(BF16)], 1
    )
    attended = jnp.concatenate([attended_near, attended_far], 0)
    grad_o = weight_grad(grad_one_all, attended)
    grad_w_qkv = weight_grad(normed_all, grad_qkv)
    grad_att = line.hold(jnp.concatenate([grad_w_qkv, grad_o], 1))
    line.mark(grad_att)
    sum_att = Scatter(split(grad_att), dp_size)
    sum_att.step(line)
    grad_qkv_bias = jnp.sum(grad_qkv.astype(F32), 0)
    grad_normed_part = mm("rf,df->rd", line.hold(grad_qkv), w_qkv)
    scaled_one = states_f * rms_one
    grad_gain_one = jnp.sum(grad_normed_part * scaled_one, 0)
    grad_normed_part = grad_normed_part.astype(BF16)
    line.mark(grad_normed_part)
    sum_last = Sum()
    sum_last.far(grad_normed_part[half:], line)
    sum_last.near(grad_normed_part[:half], line)
    sum_last.turn(line)
    sum_up.step(line)
    for _ in range(steps - 3):
        sum_att.step(line)
    sum_gate.step(line)
    grad_normed = sum_last.result()
    pulled = gain_one * grad_normed
    scaled_own = scaled_one[:row_count]
    grad_states = grad_middle + rms_one[:row_count] * (
        pulled - scaled_own * jnp.mean(pulled * scaled_own, -1, keepdims=True)
    )
    sum_att.step(line)
    sum_up.step(line)
    sum_att.step(line)

    att_sum = sum_att.result()
    qkv_sum, o_sum = att_sum[:, :qkv_cols], att_sum[:, qkv_cols:]
    grad_w_query = qkv_sum[:, :head_cols]
    kv_sum = qkv_sum[:, head_cols:].reshape(groups, shard_rows // groups, 2 * HEAD_SIZE)
    kv_rel = [lax.dynamic_index_in_dim(kv_sum, b, 0, keepdims=False) for b in blocks]
    kv_in = swap(jnp.stack([kv_rel[1], kv_rel[3]]), "tensor", 4, 1)
    kv_own = kv_rel[0] + kv_in[0]
    kv_other = swap(kv_rel[2] + kv_in[1], "tensor", 4, 2)
    first = kv_head == 0
    kv_low = jnp.where(first, kv_own, kv_other)
    kv_high = jnp.where(first, kv_other, kv_own)
    grad_w_key = jnp.concatenate([kv_low[:, :HEAD_SIZE], kv_high[:, :HEAD_SIZE]], 1)
    grad_w_value = jnp.concatenate([kv_low[:, HEAD_SIZE:], kv_high[:, HEAD_SIZE:]], 1)

    def put(length, vector, index):
        return lax.dynamic_update_slice_in_dim(jnp.zeros((length,), F32), vector, index, 0)

    kv_cols = KEY_VALUE_HEADS * HEAD_SIZE
    packed = jnp.concatenate(
        [
            put(QUERY_HEADS * HEAD_SIZE, grad_qkv_bias[:head_cols], tensor_index * head_cols),
            put(kv_cols, grad_qkv_bias[head_cols : head_cols + HEAD_SIZE], kv_head * HEAD_SIZE),
            put(kv_cols, grad_qkv_bias[head_cols + HEAD_SIZE :], kv_head * HEAD_SIZE),
            grad_gain_one,
            grad_gain_two,
            jnp.full((HEAD_SIZE,), square_sum, F32),
        ]
    )
    packed = sum_small(packed.reshape(-1, HEAD_SIZE), dp_size).reshape(-1)
    device = dp_index * groups + tensor_index
    smalls = []
    at = 0
    for width in (bias_part, kv_part, kv_part, bias_part, bias_part):
        smalls.append(lax.dynamic_slice_in_dim(packed, at + device * width, width, 0))
        at += width * dp_size * groups
    distill_loss = packed[at] / (2.0 * count_all * feature_count)
    return (
        result.astype(BF16),
        distill_loss,
        grad_states,
        grad_w_query,
        grad_w_key,
        grad_w_value,
        o_sum.T,
        sum_gate.result(),
        sum_up.result(),
        sum_down.result().T,
        smalls[0],
        smalls[1],
        smalls[2],
        smalls[3],
        smalls[4],
    )


def solution(mesh):
    rows = P(("dp", "tensor"), None)
    flat = P(("dp", "tensor"))
    return jax.shard_map(
        body,
        mesh=mesh,
        in_specs=(
            rows,
            rows,
            rows,
            P("dp"),
            P("dp", None),
            P("dp", "tensor"),
            rows,
            rows,
            P("tensor", "dp"),
            P("dp", "tensor"),
            P("dp", "tensor"),
            P("tensor", "dp"),
            flat,
            flat,
            flat,
            flat,
            flat,
        ),
        out_specs=(
            rows,
            P(),
            rows,
            P("dp", "tensor"),
            rows,
            rows,
            P("tensor", "dp"),
            P("dp", "tensor"),
            P("dp", "tensor"),
            P("tensor", "dp"),
            flat,
            flat,
            flat,
            flat,
            flat,
        ),
        check_vma=False,
    )
```
